256 devices in a mesh: dp: 8 (over z), seq: 8 (over x, core), tensor: 4 (over y).
Axes of the slice: x: 4, y: 4, z: 8, core: 2. Of those that a mesh axis runs over, the one named last changes fastest.
Arguments:
- hidden_in: bfloat16 [8192, 7168], P(('dp', 'seq'), 'tensor'), parts along dimension 0, may hold values from -6 to 6
- norm_gain: float32 [7168], P('tensor'), may hold values from 0.1 to 1.9
- expert_ids: int32 [8192, 2], P(('dp', 'seq')), parts along dimension 0, may hold values from 0 to 7, all different within a row; in each aligned block of 128 rows (0 to 127, 128 to 255, ...) at most 48 rows name the same one
- gate_weights: float32 [8192, 2], P(('dp', 'seq')), parts along dimension 0, may hold values from 0.1 to 1
- w_gate: bfloat16 [8, 7168, 1024], P('seq', None, 'tensor'), may hold values from -448 to 448, as said below
- w_up: bfloat16 [8, 7168, 1024], P('seq', None, 'tensor'), may hold values from -448 to 448, as said below
- w_down: bfloat16 [8, 1024, 7168], P('seq', None, 'tensor'), may hold values from -448 to 448, as said below
- scale_gate: float32 [8, 56, 8], P('seq', None, 'tensor'), may hold values from 4.370214e-05 to 0.00017480856
- scale_up: float32 [8, 56, 8], P('seq', None, 'tensor'), may hold values from 4.370214e-05 to 0.00017480856
- scale_down: float32 [8, 8, 56], P('seq', None, 'tensor'), may hold values from 0.000115625 to 0.0004625
Outputs:
- moe_out: bfloat16 [8192, 7168], P(('dp', 'seq'), 'tensor'), parts along dimension 0
The draws below stay inside these ranges and needn't reach their ends.
There are 8 independent parts, one for each index of `dp`. The reference program is written for one: setup_inputs(seed, part) draws one part's arguments, and reference() takes and returns one part's arrays. A program takes and returns all parts, laid end to end along the dimension named above; an argument that names none is the same for every part. Nothing has to cross between parts.
Inputs may be any that keep to these rules, and one draw needn't show every extreme that they name: `expert_ids`: each row names 2 different experts. Within the rows of one index of seq (aligned blocks of 128 rows) no expert is named by more than 48 rows, a bound that some block reaches. `w_gate`: every entry is a normal FP8 e4m3 number of magnitude 1 to 448. `w_up`: every entry is a normal FP8 e4m3 number of magnitude 1 to 448. `w_down`: every entry is a normal FP8 e4m3 number of magnitude 1 to 448.
All inputs are finite; a program needn't handle non-finite values.
Results may differ from the reference program's by a relative error of at most 0.019.
Values may be sent and summed in bfloat16 or wider, within the bound.
No kernel may reach another device: no remote copies, remote signals or barrier semaphores. Data moves between devices by JAX's collectives and lax.ppermute only.
A program may use at most 128 MiB of HBM per device.

```python
import math
import jax
import jax.numpy as jnp
import numpy as np
from jax import lax

D = 7168
BLOCK = 128
TOP = 2
TOK_SEQ = 128
EXPERTS = 8
HIDDEN_SIZE = 1024
CAP = 48
TOKENS = 1024
N_SEQ = 8


def stored_values(key, shape):
    sign = jax.random.randint(jax.random.fold_in(key, 11), shape, 0, 2) * 2 - 1
    power = jax.random.randint(jax.random.fold_in(key, 12), shape, 0, 9)
    mantissa = jax.random.randint(jax.random.fold_in(key, 13), shape, 0, 8)
    mantissa = jnp.where(power == 8, jnp.minimum(mantissa, 6), mantissa)
    magnitude = (8.0 + mantissa.astype(jnp.float32)) / 8.0 * jnp.exp2(power.astype(jnp.float32))
    return (sign.astype(jnp.float32) * magnitude).astype(jnp.bfloat16)


def draw_w_gate(key, part):
    return stored_values(jax.random.fold_in(key, 101), (EXPERTS, D, HIDDEN_SIZE))


def draw_w_up(key, part):
    return stored_values(jax.random.fold_in(key, 202), (EXPERTS, D, HIDDEN_SIZE))


def draw_w_down(key, part):
    return stored_values(jax.random.fold_in(key, 303), (EXPERTS, HIDDEN_SIZE, D))


def shard_levels(key, extent, cuts, smallest, high):
    def one(dim, blocks):
        steps = jax.random.uniform(jax.random.fold_in(jax.random.fold_in(key, 6), dim), (blocks,), jnp.float32, smallest / len(cuts), high / len(cuts))
        return jnp.repeat(jnp.exp(steps), extent[dim] // blocks).reshape((-1,) + (1,) * (len(extent) - dim - 1))

    level = one(*cuts[0])
    for cut in cuts[1:]:
        level = level * one(*cut)
    return level


def shared_out(key, own, number, rows, number_of, top, most, skew):
    ranking = jax.random.permutation(key, number_of)
    packed, ordinary = load_shares(number_of, rows * top, most, skew, True), load_shares(number_of, rows * top, most, skew, False)
    places = jnp.arange(number_of)

    def named(lengths, rotation):
        used = int((lengths > 0).sum())
        fixed = max(1, used // 4)
        moved = fixed + (places - fixed + rotation * (used - fixed)) % max(1, number_of - fixed)
        return jnp.zeros((number_of,), jnp.int32).at[ranking[jnp.where(places < fixed, places, moved)]].set(jnp.asarray(lengths, jnp.int32))

    lengths = jnp.where(number % 4 == 0, named(packed, number // 4), named(ordinary, number - number // 4 - 1))
    mixed = jax.random.permutation(jax.random.fold_in(own, 3), number_of)
    giver, sink = mixed[0:number_of // 2 * 2:2], mixed[1:number_of // 2 * 2:2]
    slack = jnp.minimum(lengths[giver] - 1, most - lengths[sink]) // 2
    slack = jnp.where((giver == ranking[0]) | (sink == ranking[0]) | (lengths[sink] == 0), 0, jnp.maximum(slack, 0))
    moved = jax.random.randint(jax.random.fold_in(own, 4), (number_of // 2,), 0, 1 << 20) % (slack + 1)
    lengths = lengths.at[giver].add(-moved).at[sink].add(moved)
    items = jnp.searchsorted(jnp.cumsum(lengths), jnp.arange(rows * top), side="right").astype(jnp.int32)
    listing = items.reshape(top, rows).T
    listing = listing[jax.random.permutation(jax.random.fold_in(own, 1), rows)]
    rotation = jax.random.randint(jax.random.fold_in(own, 2), (rows, 1), 0, top)
    return jnp.take_along_axis(listing, (jnp.arange(top)[None, :] + rotation) % top, axis=1)


def load_shares(count, total, limit, slope, full):
    weights = [(1 << 20) // math.isqrt(grade ** slope) + 1 for grade in range(1, count + 1)]
    largest = limit if full else min(limit, max(-(-total // count), total * weights[0] // sum(weights)))
    least = 1 if total - largest >= count - 1 else 0
    counts, surplus = [largest] + [least] * (count - 1), total - largest - least * (count - 1)
    while surplus > 0:
        movable = [i for i in range(1, count) if counts[i] < largest] or [i for i in range(1, count) if counts[i] < limit]
        pool, left = sum([weights[i] for i in movable]), surplus
        for i in movable:
            more = min(limit - counts[i], max(1, left * weights[i] // pool), surplus)
            counts[i] = counts[i] + more
            surplus = surplus - more
    return np.array(counts)


def normal_values(rng, dims, scale, reach, shards=(), held_as=jnp.bfloat16):
    drawn = jax.random.normal(rng, dims, jnp.float32) * scale
    if len(shards) > 0:
        drawn = shard_levels(rng, dims, shards, -0.22, 0.18) * drawn
    return jnp.clip(drawn, min=-reach, max=reach).astype(held_as)


def setup_inputs(seed: int = 0, part: int = 0) -> dict:
    keys = jax.random.split(jax.random.key(seed), 11)
    part_splits = jax.random.split(jax.random.fold_in(keys[10], part), 11)
    hidden_in = normal_values(part_splits[0], (TOKENS, D), 1.0, 6.0, ((0, 8), (1, 4)))
    norm_gain = jnp.clip(1.0 + 0.18 * jax.random.normal(keys[1], (D,), jnp.float32), 0.1, 1.9)
    expert_ids_keys = jax.random.split(jax.random.fold_in(part_splits[2], 1), TOKENS // TOK_SEQ)
    expert_ids_turns = jax.random.permutation(jax.random.fold_in(part_splits[2], 3), TOKENS // TOK_SEQ)
    expert_ids = jax.vmap(lambda own, number: shared_out(jax.random.fold_in(part_splits[2], 2), own, number, TOK_SEQ, EXPERTS, TOP, CAP, 2))(expert_ids_keys, expert_ids_turns).reshape((TOKENS, TOP))
    gate_weights = jnp.clip(jnp.exp(math.log(1.0) - 2.3025851 * jax.random.uniform(part_splits[3], (TOKENS, TOP), jnp.float32) ** shard_levels(part_splits[3], (TOKENS, TOP), ((0, 8),), -0.2, 0.2)), 0.1, 1.0)
    w_gate = draw_w_gate(jax.random.fold_in(keys[10], 71), part)
    w_up = draw_w_up(jax.random.fold_in(keys[10], 71), part)
    w_down = draw_w_down(jax.random.fold_in(keys[10], 71), part)
    scale_gate = jnp.clip(jnp.exp(math.log(0.00017480856) - 1.3862944 * jax.random.uniform(keys[7], (EXPERTS, D // BLOCK, HIDDEN_SIZE // BLOCK), jnp.float32) ** shard_levels(keys[7], (EXPERTS, D // BLOCK, HIDDEN_SIZE // BLOCK), ((0, 8), (2, 4)), -0.2, 0.2)), 4.3702140828827396e-05, 0.00017480856)
    scale_up = jnp.clip(jnp.exp(math.log(0.00017480856) - 1.3862944 * jax.random.uniform(keys[8], (EXPERTS, D // BLOCK, HIDDEN_SIZE // BLOCK), jnp.float32) ** shard_levels(keys[8], (EXPERTS, D // BLOCK, HIDDEN_SIZE // BLOCK), ((0, 8), (2, 4)), -0.2, 0.2)), 4.3702140828827396e-05, 0.00017480856)
    scale_down = jnp.clip(jnp.exp(math.log(0.0004625) - 1.3862944 * jax.random.uniform(keys[9], (EXPERTS, HIDDEN_SIZE // BLOCK, D // BLOCK), jnp.float32) ** shard_levels(keys[9], (EXPERTS, HIDDEN_SIZE // BLOCK, D // BLOCK), ((0, 8), (2, 4)), -0.2, 0.2)), 0.000115625, 0.0004625)
    return {"hidden_in": hidden_in, "norm_gain": norm_gain, "expert_ids": expert_ids, "gate_weights": gate_weights, "w_gate": w_gate, "w_up": w_up, "w_down": w_down, "scale_gate": scale_gate, "scale_up": scale_up, "scale_down": scale_down}


def dequant(values, scales):
    row_count, col_count = values.shape
    row_blocks, col_blocks = scales.shape
    shaped = values.astype(jnp.float32).reshape(row_blocks, row_count // row_blocks, col_blocks, col_count // col_blocks)
    return (shaped * scales[:, None, :, None]).reshape(row_count, col_count).astype(jnp.bfloat16)

def reference(hidden_in, norm_gain, expert_ids, gate_weights, w_gate, w_up, w_down, scale_gate, scale_up, scale_down):
    as_float = hidden_in.astype(jnp.float32)
    inverse = lax.rsqrt(lax.optimization_barrier(jnp.sum(as_float * as_float, axis=1, keepdims=True)) / D + 1e-06)
    normed = as_float * inverse * norm_gain[None, :]
    blocks = normed.reshape(TOKENS, D // BLOCK, BLOCK)
    act_scale = ((lax.optimization_barrier(jnp.max(jnp.abs(blocks), axis=2)) + 1e-06) / 448.0).astype(jnp.bfloat16)
    act_q = (blocks / act_scale.astype(jnp.float32)[:, :, None]).astype(jnp.bfloat16)
    x_deq = (act_q.astype(jnp.float32) * act_scale.astype(jnp.float32)[:, :, None]).astype(jnp.bfloat16).reshape(TOKENS, D)
    flat_ids = expert_ids.reshape(N_SEQ, TOK_SEQ * TOP).astype(jnp.int32)
    onehot = (flat_ids[:, :, None] == jnp.arange(EXPERTS, dtype=jnp.int32)[None, None, :]).astype(jnp.int32)
    before = jnp.cumsum(onehot, axis=1) - onehot
    position = lax.optimization_barrier(jnp.sum(before * onehot, axis=2)).astype(jnp.int32)
    shard_index = jnp.broadcast_to(jnp.arange(N_SEQ, dtype=jnp.int32)[:, None], flat_ids.shape)
    assign_index = jnp.broadcast_to(jnp.arange(TOK_SEQ * TOP, dtype=jnp.int32)[None, :], flat_ids.shape)
    token_index = (shard_index * TOK_SEQ + assign_index // TOP).astype(jnp.int32)
    slot_token = jnp.zeros((EXPERTS, N_SEQ, CAP), jnp.int32).at[flat_ids, shard_index, position].set(token_index)
    slot_gate = jnp.zeros((EXPERTS, N_SEQ, CAP), jnp.float32).at[flat_ids, shard_index, position].set(gate_weights.reshape(N_SEQ, TOK_SEQ * TOP).astype(jnp.float32))

    def one_expert(running, expert):
        tokens_here = slot_token[expert].reshape(-1)
        gains_here = slot_gate[expert].reshape(-1)
        rows_here = x_deq[tokens_here]
        gate_deq = dequant(w_gate[expert], scale_gate[expert])
        up_deq = dequant(w_up[expert], scale_up[expert])
        down_deq = dequant(w_down[expert], scale_down[expert])
        gate_act = jnp.dot(rows_here, gate_deq, preferred_element_type=jnp.float32)
        up_act = jnp.dot(rows_here, up_deq, preferred_element_type=jnp.float32)
        hidden = (jax.nn.silu(gate_act) * up_act).astype(jnp.bfloat16)
        outputs = jnp.dot(hidden, down_deq, preferred_element_type=jnp.float32).astype(jnp.bfloat16)
        weighted = outputs.astype(jnp.float32) * gains_here[:, None]
        return (running.at[tokens_here].add(weighted), None)
    summed, unused = lax.scan(one_expert, jnp.zeros((TOKENS, D), jnp.float32), jnp.arange(EXPERTS, dtype=jnp.int32))
    return summed.astype(jnp.bfloat16)
```

```python
import functools

import jax
import jax.numpy as jnp
from jax import lax
from jax.experimental import pallas as pl
from jax.experimental.pallas import tpu as pltpu
from jax.sharding import PartitionSpec as P

D = 7168
BLOCK = 128
N_EXP = 8
CAP = 48
SLOTS = N_EXP * CAP
TOK = 128
WIDTH = 1792
PW = 1152
QW = WIDTH - PW
HID = 256
ALL_HID = 1024
F32 = jnp.float32
BF16 = jnp.bfloat16


def full(shape):
    return pl.BlockSpec(shape, lambda: (0,) * len(shape))


def split3(v):
    hi = v.astype(BF16).astype(F32)
    mid = (v - hi).astype(BF16).astype(F32)
    lo = (v - hi - mid).astype(BF16).astype(F32)
    return hi, mid, lo


def lanes3(v):
    hi, mid, lo = split3(v)
    lane = lax.broadcasted_iota(jnp.int32, (v.shape[0], BLOCK), 1)
    packed = jnp.where(lane == 0, hi, jnp.where(lane == 1, mid, jnp.where(lane == 2, lo, 0.0)))
    return packed.astype(BF16)


def picker_of(ids):
    expert = lax.broadcasted_iota(jnp.int32, (N_EXP, TOK), 0)
    named = ((ids[0:1, :] == expert) | (ids[1:2, :] == expert)).astype(F32)
    row = lax.broadcasted_iota(jnp.int32, (TOK, TOK), 0)
    col = lax.broadcasted_iota(jnp.int32, (TOK, TOK), 1)
    earlier = (row < col).astype(F32)
    position = jnp.dot(named.astype(BF16), earlier.astype(BF16), preferred_element_type=F32)
    slot = lax.broadcasted_iota(jnp.int32, (CAP, TOK), 0).astype(F32)
    parts = []
    for e in range(N_EXP):
        hit = (slot == position[e : e + 1, :]) & (named[e : e + 1, :] > 0.5)
        parts.append(hit.astype(F32))
    return jnp.concatenate(parts, axis=0)


def source_kernel(ids_ref, x_ref, gain_ref, send_ref, q_ref, picker_ref, xq):
    squares = jnp.zeros((TOK, BLOCK), F32)
    for b in range(WIDTH // BLOCK):
        cols = slice(b * BLOCK, (b + 1) * BLOCK)
        x = x_ref[:, cols].astype(F32)
        squares = squares + x * x
        scaled = x * gain_ref[:, cols]
        top = jnp.max(jnp.abs(scaled), axis=1, keepdims=True)
        scale = ((top + 1e-06) / 448.0).astype(BF16).astype(F32)
        quant = (scaled / scale).astype(BF16).astype(F32)
        value = (quant * scale).astype(BF16)
        if b * BLOCK < PW:
            xq[:, cols] = value
        else:
            q_ref[:, b * BLOCK - PW : (b + 1) * BLOCK - PW] = value
    q_ref[:, QW:] = lanes3(jnp.sum(squares, axis=1, keepdims=True))
    picker = picker_of(ids_ref[...]).astype(BF16)
    picker_ref[...] = picker
    send_ref[...] = jnp.dot(picker, xq[...], preferred_element_type=F32).astype(BF16)


def source(ids, x, gain):
    return pl.pallas_call(
        source_kernel,
        out_shape=(
            jax.ShapeDtypeStruct((SLOTS, PW), BF16),
            jax.ShapeDtypeStruct((TOK, QW + BLOCK), BF16),
            jax.ShapeDtypeStruct((SLOTS, TOK), BF16),
        ),
        in_specs=[full((2, TOK)), full((TOK, WIDTH)), full((1, WIDTH))],
        out_specs=(full((SLOTS, PW)), full((TOK, QW + BLOCK)), full((SLOTS, TOK))),
        scratch_shapes=[pltpu.VMEM((TOK, PW), BF16)],
        name="source",
    )(ids, x, gain)


def route_kernel(picker_ref, q0, q1, q2, q3, out_ref):
    total = jnp.zeros((TOK, BLOCK), F32)
    picker = picker_ref[...]
    for r, q in enumerate((q0, q1, q2, q3)):
        out_ref[:, r * QW : (r + 1) * QW] = jnp.dot(
            picker, q[:, :QW], preferred_element_type=F32
        ).astype(BF16)
        total = total + q[:, QW:].astype(F32)
    squares = lanes3(jnp.sum(total, axis=1, keepdims=True))
    out_ref[:, 4 * QW :] = jnp.dot(picker, squares, preferred_element_type=F32).astype(BF16)


def route(picker, pieces):
    wide = 4 * QW + BLOCK
    return pl.pallas_call(
        route_kernel,
        out_shape=jax.ShapeDtypeStruct((SLOTS, wide), BF16),
        in_specs=[full((SLOTS, TOK))] + [full((TOK, QW + BLOCK))] * 4,
        out_specs=full((SLOTS, wide)),
        name="route",
    )(picker, *pieces)


def dequant_up_kernel(scale_gate, scale_up, gate_ref, up_ref, out_ref):
    i = pl.program_id(0)
    for b in range(7):
        rows = slice(b * BLOCK, (b + 1) * BLOCK)
        for c in range(2):
            cols = slice(c * BLOCK, (c + 1) * BLOCK)
            shifted = slice(HID + c * BLOCK, HID + (c + 1) * BLOCK)
            gate = gate_ref[rows, cols].astype(F32) * scale_gate[c, i * 7 + b]
            out_ref[rows, cols] = gate.astype(BF16)
            up = up_ref[rows, cols].astype(F32) * scale_up[c, i * 7 + b]
            out_ref[rows, shifted] = up.astype(BF16)


def dequant_up(scale_gate, scale_up, gate, up):
    rows = 7 * BLOCK
    smem = pl.BlockSpec(memory_space=pltpu.SMEM)
    return pl.pallas_call(
        dequant_up_kernel,
        grid=(D // rows,),
        out_shape=jax.ShapeDtypeStruct((D, 2 * HID), BF16),
        in_specs=[
            smem,
            smem,
            pl.BlockSpec((rows, HID), lambda i: (i, 0)),
            pl.BlockSpec((rows, HID), lambda i: (i, 0)),
        ],
        out_specs=pl.BlockSpec((rows, 2 * HID), lambda i: (i, 0)),
        name="dequant_up",
    )(scale_gate, scale_up, gate, up)


def dequant_down_kernel(scale, w_ref, out_ref):
    i = pl.program_id(0)
    for c in range(WIDTH // BLOCK):
        cols = slice(c * BLOCK, (c + 1) * BLOCK)
        out_ref[:, cols] = (w_ref[:, cols].astype(F32) * scale[i, c]).astype(BF16)


def dequant_down(scale, w):
    return pl.pallas_call(
        dequant_down_kernel,
        grid=(ALL_HID // BLOCK,),
        out_shape=jax.ShapeDtypeStruct((ALL_HID, WIDTH), BF16),
        in_specs=[
            pl.BlockSpec(memory_space=pltpu.SMEM),
            pl.BlockSpec((BLOCK, WIDTH), lambda i: (i, 0)),
        ],
        out_specs=pl.BlockSpec((BLOCK, WIDTH), lambda i: (i, 0)),
        name="dequant_down",
    )(scale, w)


def combine_prep_kernel(ids_ref, gates_ref, picker_ref, sel_ref, weight_ref):
    picker = picker_ref[...].astype(F32)
    for k in range(2):
        parts = []
        for e in range(N_EXP):
            mine = (ids_ref[k : k + 1, :] == e).astype(F32)
            parts.append(picker[e * CAP : (e + 1) * CAP, :] * mine)
        chosen = jnp.concatenate(parts, axis=0)
        sel_ref[k] = jnp.transpose(chosen).astype(BF16)
        weight_ref[k] = jnp.transpose(jnp.broadcast_to(gates_ref[k : k + 1, :], (TOK, TOK)))


def combine_prep(ids, gates, picker):
    return pl.pallas_call(
        combine_prep_kernel,
        out_shape=(
            jax.ShapeDtypeStruct((2, TOK, SLOTS), BF16),
            jax.ShapeDtypeStruct((2, TOK, TOK), F32),
        ),
        in_specs=[full((2, TOK)), full((2, TOK)), full((SLOTS, TOK))],
        out_specs=(full((2, TOK, SLOTS)), full((2, TOK, TOK))),
        name="combine_prep",
    )(ids, gates, picker)


def hidden_kernel(me_ref, p0, p1, p2, p3a, p3b, q, w_hbm, out_ref, wbuf, acc, sems):
    me = me_ref[0]
    copies = []
    offset = 0
    for part, (start, size) in enumerate(((0, PW), (PW, QW))):
        for r, shift in enumerate((0, 3, 1, 2)):
            owner = lax.rem(me + shift, 4)
            row = pl.multiple_of(owner * WIDTH + start, BLOCK)
            copy = pltpu.make_async_copy(
                w_hbm.at[pl.ds(row, size)], wbuf.at[pl.ds(offset, size)], sems.at[len(copies)]
            )
            copy.start()
            copies.append((copy, offset, size))
            offset += size

    def weights(n):
        copy, offset, size = copies[n]
        copy.wait()
        return wbuf[offset : offset + size, :]

    acc[...] = jnp.dot(p0[...], weights(0), preferred_element_type=F32)
    acc[...] += jnp.dot(p1[...], weights(1), preferred_element_type=F32)
    acc[...] += jnp.dot(p2[...], weights(2), preferred_element_type=F32)
    w = weights(3)
    half = SLOTS // 2
    acc[:half] += jnp.dot(p3a[...], w, preferred_element_type=F32)
    acc[half:] += jnp.dot(p3b[...], w, preferred_element_type=F32)
    for r in range(4):
        acc[...] += jnp.dot(
            q[:, r * QW : (r + 1) * QW], weights(4 + r), preferred_element_type=F32
        )
    squares = jnp.sum(q[:, 4 * QW :].astype(F32), axis=1, keepdims=True)
    inverse = lax.rsqrt(squares / D + 1e-06)
    gate = acc[:, :HID] * inverse
    up = acc[:, HID:] * inverse
    out_ref[...] = (gate / (1.0 + jnp.exp(-gate)) * up).astype(BF16)


def hidden_of(me, pieces, q, w):
    half = SLOTS // 2
    return pl.pallas_call(
        hidden_kernel,
        out_shape=jax.ShapeDtypeStruct((SLOTS, HID), BF16),
        in_specs=[pl.BlockSpec(memory_space=pltpu.SMEM)]
        + [full((SLOTS, PW))] * 3
        + [full((half, PW))] * 2
        + [full((SLOTS, 4 * QW + BLOCK)), pl.BlockSpec(memory_space=pl.ANY)],
        out_specs=full((SLOTS, HID)),
        scratch_shapes=[
            pltpu.VMEM((D, 2 * HID), BF16),
            pltpu.VMEM((SLOTS, 2 * HID), F32),
            pltpu.SemaphoreType.DMA((8,)),
        ],
        name="hidden",
    )(me, *pieces, q, w)


def down_kernel(me_ref, h0, h1, h2, h3a, h3b, w_ref, out_ref):
    me = me_ref[0]
    half = SLOTS // 2

    def weights(shift):
        owner = lax.rem(me + shift, 4)
        return w_ref[pl.ds(pl.multiple_of(owner * HID, HID), HID), :]

    last = jnp.concatenate([h3a[...], h3b[...]], axis=0)
    total = jnp.dot(h0[...], weights(0), preferred_element_type=F32)
    total += jnp.dot(h1[...], weights(3), preferred_element_type=F32)
    total += jnp.dot(h2[...], weights(1), preferred_element_type=F32)
    total += jnp.dot(last, weights(2), preferred_element_type=F32)
    out_ref[...] = total.astype(BF16)


def down_of(me, pieces, w):
    half = SLOTS // 2
    return pl.pallas_call(
        down_kernel,
        out_shape=jax.ShapeDtypeStruct((SLOTS, WIDTH), BF16),
        in_specs=[pl.BlockSpec(memory_space=pltpu.SMEM)]
        + [full((SLOTS, HID))] * 3
        + [full((half, HID))] * 2
        + [full((ALL_HID, WIDTH))],
        out_specs=full((SLOTS, WIDTH)),
        name="down",
    )(me, *pieces, w)


def combine_kernel(sel_ref, weight_ref, x_ref, out_ref):
    x = x_ref[...]
    first = jnp.dot(sel_ref[0], x, preferred_element_type=F32)
    second = jnp.dot(sel_ref[1], x, preferred_element_type=F32)
    for c in range(WIDTH // BLOCK):
        cols = slice(c * BLOCK, (c + 1) * BLOCK)
        out_ref[:, cols] = (
            weight_ref[0] * first[:, cols] + weight_ref[1] * second[:, cols]
        ).astype(BF16)


def combine(sel, weight, x):
    return pl.pallas_call(
        combine_kernel,
        out_shape=jax.ShapeDtypeStruct((TOK, WIDTH), BF16),
        in_specs=[full((2, TOK, SLOTS)), full((2, TOK, TOK)), full((SLOTS, WIDTH))],
        out_specs=full((TOK, WIDTH)),
        name="combine",
    )(sel, weight, x)


def shift(x, step):
    return lax.ppermute(x, "tensor", [(i, (i + step) % 4) for i in range(4)])


def spread(x):
    half = x.shape[0] // 2
    low, high = shift(x, 1), shift(x, 3)
    return low, high, shift(low[:half], 1), shift(high[half:], 3)


def exchange(x):
    sized = x.reshape(N_EXP, CAP, x.shape[1])
    return lax.all_to_all(sized, "seq", split_axis=0, concat_axis=0, tiled=True).reshape(x.shape)


def local(
    hidden_in,
    norm_gain,
    expert_ids,
    gate_weights,
    w_gate,
    w_up,
    w_down,
    scale_gate,
    scale_up,
    scale_down,
):
    me = lax.axis_index("tensor").astype(jnp.int32).reshape(1)
    ids = expert_ids.T
    send, q, picker = source(ids, hidden_in, norm_gain.reshape(1, WIDTH))
    q_pieces = (q, shift(q, 1), shift(q, 3), shift(q, 2))
    mine = exchange(send)
    routed = route(picker, q_pieces)
    got_q = exchange(routed)
    pieces = (mine,) + spread(mine)
    w_both = dequant_up(scale_gate[0].T, scale_up[0].T, w_gate[0], w_up[0])
    w_out = dequant_down(scale_down[0], w_down[0])
    sel, weight = combine_prep(ids, gate_weights.T, picker)
    hidden = hidden_of(me, pieces, got_q, w_both)
    outputs = down_of(me, (hidden,) + spread(hidden), w_out)
    returned = exchange(outputs)
    return combine(sel, weight, returned)


def solution(mesh):
    in_specs = (
        P(("dp", "seq"), "tensor"),
        P("tensor"),
        P(("dp", "seq"), None),
        P(("dp", "seq"), None),
        P("seq", None, "tensor"),
        P("seq", None, "tensor"),
        P("seq", None, "tensor"),
        P("seq", None, "tensor"),
        P("seq", None, "tensor"),
        P("seq", None, "tensor"),
    )
    out_specs = P(("dp", "seq"), "tensor")
    return jax.shard_map(local, mesh=mesh, in_specs=in_specs, out_specs=out_specs, check_vma=False)
```

```python
import functools

import jax
import jax.numpy as jnp
from jax import lax
from jax.experimental import pallas as pl
from jax.experimental.pallas import tpu as pltpu
from jax.sharding import PartitionSpec as P

D = 7168
BLOCK = 128
N_EXP = 8
CAP = 48
SLOTS = N_EXP * CAP
TOK = 128
WIDTH = 1792
PW = 1152
QW = WIDTH - PW
HALF = SLOTS // 2
HID = 256
ALL_HID = 1024
F32 = jnp.float32
BF16 = jnp.bfloat16


def full():
    return pl.BlockSpec(memory_space=pltpu.VMEM)


def whole(shape):
    return pl.BlockSpec(shape, lambda: (0,) * len(shape))


def near(x):
    return pltpu.with_memory_space_constraint(x, pltpu.VMEM)


def load(pairs, sems):
    copies = [pltpu.make_async_copy(src, dst, sems.at[n]) for n, (src, dst) in enumerate(pairs)]
    for copy in copies:
        copy.start()
    return copies


HERE = pl.BlockSpec(memory_space=pl.ANY)
SCALAR = pl.BlockSpec(memory_space=pltpu.SMEM)


def limit(mib):
    return pltpu.CompilerParams(vmem_limit_bytes=mib << 20)


def split3(v):
    hi = v.astype(BF16).astype(F32)
    mid = (v - hi).astype(BF16).astype(F32)
    lo = (v - hi - mid).astype(BF16).astype(F32)
    return hi, mid, lo


def lanes3(v):
    hi, mid, lo = split3(v)
    lane = lax.broadcasted_iota(jnp.int32, (v.shape[0], BLOCK), 1)
    packed = jnp.where(lane == 0, hi, jnp.where(lane == 1, mid, jnp.where(lane == 2, lo, 0.0)))
    return packed.astype(BF16)


def picker_of(ids):
    expert = lax.broadcasted_iota(jnp.int32, (N_EXP, TOK), 0)
    named = ((ids[0:1, :] == expert) | (ids[1:2, :] == expert)).astype(F32)
    row = lax.broadcasted_iota(jnp.int32, (TOK, TOK), 0)
    col = lax.broadcasted_iota(jnp.int32, (TOK, TOK), 1)
    earlier = (row < col).astype(F32)
    position = jnp.dot(named.astype(BF16), earlier.astype(BF16), preferred_element_type=F32)
    slot = lax.broadcasted_iota(jnp.int32, (CAP, TOK), 0).astype(F32)
    parts = []
    for e in range(N_EXP):
        hit = (slot == position[e : e + 1, :]) & (named[e : e + 1, :] > 0.5)
        parts.append(hit.astype(F32))
    return jnp.concatenate(parts, axis=0)


def source_kernel(ids_ref, x_ref, gain_ref, send_ref, q_ref, picker_ref, xq):
    picker = picker_of(ids_ref[...]).astype(BF16)
    picker_ref[...] = picker
    squares = jnp.zeros((TOK, BLOCK), F32)
    for b in range(WIDTH // BLOCK):
        cols = slice(b * BLOCK, (b + 1) * BLOCK)
        x = x_ref[:, cols].astype(F32)
        squares = squares + x * x
        scaled = x * gain_ref[cols].reshape(1, BLOCK)
        top = jnp.max(jnp.abs(scaled), axis=1, keepdims=True)
        scale = ((top + 1e-06) / 448.0).astype(BF16).astype(F32)
        quant = (scaled / scale).astype(BF16).astype(F32)
        value = (quant * scale).astype(BF16)
        if b * BLOCK < PW:
            xq[:, cols] = value
        else:
            q_ref[:, b * BLOCK - PW : (b + 1) * BLOCK - PW] = value
    q_ref[:, QW:] = lanes3(jnp.sum(squares, axis=1, keepdims=True))
    send_ref[...] = jnp.dot(picker, xq[...], preferred_element_type=F32).astype(BF16)


def source(ids, x, gain):
    return pl.pallas_call(
        source_kernel,
        out_shape=(
            jax.ShapeDtypeStruct((SLOTS, PW), BF16),
            jax.ShapeDtypeStruct((TOK, QW + BLOCK), BF16),
            jax.ShapeDtypeStruct((SLOTS, TOK), BF16),
        ),
        in_specs=[whole((2, TOK)), whole((TOK, WIDTH)), whole((WIDTH,))],
        out_specs=(whole((SLOTS, PW)), whole((TOK, QW + BLOCK)), whole((SLOTS, TOK))),
        scratch_shapes=[pltpu.VMEM((TOK, PW), BF16)],
        name="source",
    )(ids, x, gain)


def route_kernel(picker_ref, q0, q1, q2, q3, out_hbm, out_ref, sems):
    total = jnp.zeros((TOK, BLOCK), F32)
    picker = picker_ref[...]
    copies = []

    def ship(start, size):
        cols = slice(start, start + size)
        copy = pltpu.make_async_copy(
            out_ref.at[:, cols], out_hbm.at[:, cols], sems.at[len(copies)]
        )
        copy.start()
        copies.append(copy)

    for r, q in enumerate((q0, q1, q2, q3)):
        out_ref[:, r * QW : (r + 1) * QW] = jnp.dot(
            picker, q[:, :QW], preferred_element_type=F32
        ).astype(BF16)
        ship(r * QW, QW)
        total = total + q[:, QW:].astype(F32)
    squares = lanes3(jnp.sum(total, axis=1, keepdims=True))
    out_ref[:, 4 * QW :] = jnp.dot(picker, squares, preferred_element_type=F32).astype(BF16)
    ship(4 * QW, BLOCK)
    for copy in copies:
        copy.wait()


def route(picker, pieces):
    wide = 4 * QW + BLOCK
    return pl.pallas_call(
        route_kernel,
        out_shape=jax.ShapeDtypeStruct((SLOTS, wide), BF16),
        in_specs=[full()] * 5,
        out_specs=HERE,
        scratch_shapes=[pltpu.VMEM((SLOTS, wide), BF16), pltpu.SemaphoreType.DMA((5,))],
        name="route",
    )(picker, *pieces)


def rows_kernel(start, x_ref, out_ref):
    out_ref[...] = x_ref[start : start + HALF, :]


def rows_of(x, start):
    return pl.pallas_call(
        functools.partial(rows_kernel, start),
        out_shape=jax.ShapeDtypeStruct((HALF, x.shape[1]), x.dtype),
        in_specs=[full()],
        out_specs=full(),
        name="rows",
        compiler_params=limit(58),
    )(x)


def dequant_up_kernel(scale_gate, scale_up, gate_ref, up_ref, out_ref):
    i = pl.program_id(0)
    for b in range(7):
        rows = slice(b * BLOCK, (b + 1) * BLOCK)
        for c in range(2):
            cols = slice(c * BLOCK, (c + 1) * BLOCK)
            shifted = slice(HID + c * BLOCK, HID + (c + 1) * BLOCK)
            gate = gate_ref[rows, cols].astype(F32) * scale_gate[c, i * 7 + b]
            out_ref[rows, cols] = gate.astype(BF16)
            up = up_ref[rows, cols].astype(F32) * scale_up[c, i * 7 + b]
            out_ref[rows, shifted] = up.astype(BF16)


def dequant_up(scale_gate, scale_up, gate, up):
    rows = 7 * BLOCK
    smem = pl.BlockSpec(memory_space=pltpu.SMEM)
    return pl.pallas_call(
        dequant_up_kernel,
        grid=(D // rows,),
        out_shape=jax.ShapeDtypeStruct((D, 2 * HID), BF16),
        in_specs=[
            smem,
            smem,
            pl.BlockSpec((rows, HID), lambda i: (i, 0)),
            pl.BlockSpec((rows, HID), lambda i: (i, 0)),
        ],
        out_specs=pl.BlockSpec((rows, 2 * HID), lambda i: (i, 0)),
        name="dequant_up",
        compiler_params=limit(58),
    )(scale_gate, scale_up, gate, up)


def dequant_down_kernel(scale, w_ref, out_ref):
    i = pl.program_id(0)
    for c in range(WIDTH // BLOCK):
        cols = slice(c * BLOCK, (c + 1) * BLOCK)
        out_ref[:, cols] = (w_ref[:, cols].astype(F32) * scale[i, c]).astype(BF16)


def dequant_down(scale, w):
    return pl.pallas_call(
        dequant_down_kernel,
        grid=(ALL_HID // BLOCK,),
        out_shape=jax.ShapeDtypeStruct((ALL_HID, WIDTH), BF16),
        in_specs=[
            pl.BlockSpec(memory_space=pltpu.SMEM),
            pl.BlockSpec((BLOCK, WIDTH), lambda i: (i, 0)),
        ],
        out_specs=pl.BlockSpec((BLOCK, WIDTH), lambda i: (i, 0)),
        name="dequant_down",
    )(scale, w)


def combine_prep_kernel(ids_ref, gates_ref, picker_ref, sel_ref, weight_ref):
    picker = picker_ref[...].astype(F32)
    for k in range(2):
        parts = []
        for e in range(N_EXP):
            mine = (ids_ref[k : k + 1, :] == e).astype(F32)
            parts.append(picker[e * CAP : (e + 1) * CAP, :] * mine)
        chosen = jnp.concatenate(parts, axis=0)
        sel_ref[k] = jnp.transpose(chosen).astype(BF16)
        weight_ref[k] = jnp.transpose(jnp.broadcast_to(gates_ref[k : k + 1, :], (TOK, TOK)))


def combine_prep(ids, gates, picker):
    return pl.pallas_call(
        combine_prep_kernel,
        out_shape=(
            jax.ShapeDtypeStruct((2, TOK, SLOTS), BF16),
            jax.ShapeDtypeStruct((2, TOK, TOK), F32),
        ),
        in_specs=[full(), full(), full()],
        out_specs=(full(), full()),
        name="combine_prep",
    )(ids, gates, picker)


def weight_copies(me, parts, w_hbm, w_ref):
    pairs, row = [], 0
    for shift, start, size in parts:
        source_row = pl.multiple_of(lax.rem(me + shift, 4) * WIDTH + start, BLOCK)
        pairs.append((w_hbm.at[pl.ds(source_row, size)], w_ref.at[pl.ds(row, size)]))
        row += size
    return pairs


def first_kernel(me_ref, p0, p1, p2, w_hbm, acc_ref, w_ref, sems):
    parts = [(shift, 0, PW) for shift in (0, 3, 1)]
    copies = load(weight_copies(me_ref[0], parts, w_hbm, w_ref), sems)
    for copy in copies:
        copy.wait()
    total = jnp.dot(p0[...], w_ref[:PW, :], preferred_element_type=F32)
    total += jnp.dot(p1[...], w_ref[PW : 2 * PW, :], preferred_element_type=F32)
    total += jnp.dot(p2[...], w_ref[2 * PW :, :], preferred_element_type=F32)
    acc_ref[...] = total


def first_part(me, p0, p1, p2, w):
    return pl.pallas_call(
        first_kernel,
        out_shape=jax.ShapeDtypeStruct((SLOTS, 2 * HID), F32),
        in_specs=[SCALAR] + [full()] * 3 + [HERE],
        out_specs=whole((SLOTS, 2 * HID)),
        scratch_shapes=[pltpu.VMEM((3 * PW, 2 * HID), BF16), pltpu.SemaphoreType.DMA((3,))],
        name="first_part",
        compiler_params=limit(58),
    )(me, p0, p1, p2, w)


def hidden_kernel(me_ref, q, p3a, p3b, acc_hbm, w_hbm, out_ref, acc_ref, w_ref, sems):
    parts = [(2, 0, PW)] + [(shift, PW, QW) for shift in (0, 3, 1, 2)]
    pairs = weight_copies(me_ref[0], parts, w_hbm, w_ref)
    copies = load([(acc_hbm, acc_ref)] + pairs, sems)
    squares = jnp.sum(q[:, 4 * QW :].astype(F32), axis=1, keepdims=True)
    inverse = jnp.broadcast_to(lax.rsqrt(squares / D + 1e-06), (SLOTS, BLOCK))
    copies[0].wait()
    copies[1].wait()
    w_far = w_ref[:PW, :]
    acc_ref[:HALF, :] += jnp.dot(p3a[...], w_far, preferred_element_type=F32)
    acc_ref[HALF:, :] += jnp.dot(p3b[...], w_far, preferred_element_type=F32)
    for copy in copies[2:]:
        copy.wait()
    total = acc_ref[...] + jnp.dot(q[:, : 4 * QW], w_ref[PW:, :], preferred_element_type=F32)
    for c in range(HID // BLOCK):
        gate = total[:, c * BLOCK : (c + 1) * BLOCK] * inverse
        up = total[:, HID + c * BLOCK : HID + (c + 1) * BLOCK] * inverse
        value = gate / (1.0 + jnp.exp(-gate)) * up
        out_ref[:, c * BLOCK : (c + 1) * BLOCK] = value.astype(BF16)


def hidden_of(me, q, p3a, p3b, acc, w):
    return pl.pallas_call(
        hidden_kernel,
        out_shape=jax.ShapeDtypeStruct((SLOTS, HID), BF16),
        in_specs=[SCALAR] + [full()] * 3 + [HERE] * 2,
        out_specs=full(),
        scratch_shapes=[
            pltpu.VMEM((SLOTS, 2 * HID), F32),
            pltpu.VMEM((4 * QW + PW, 2 * HID), BF16),
            pltpu.SemaphoreType.DMA((6,)),
        ],
        name="hidden",
        compiler_params=limit(58),
    )(me, q, p3a, p3b, acc, w)


def down_kernel(me_ref, h0, h1, h2, h3, w_hbm, out_ref, w_ref, sems):
    me = me_ref[0]
    pairs = []
    for n, shift in enumerate((0, 3, 1, 2)):
        row = pl.multiple_of(lax.rem(me + shift, 4) * HID, HID)
        pairs.append((w_hbm.at[pl.ds(row, HID)], w_ref.at[pl.ds(n * HID, HID)]))
    copies = load(pairs, sems)
    total = None
    for n, h in enumerate((h0, h1, h2, h3)):
        copies[n].wait()
        part = jnp.dot(h[...], w_ref[n * HID : (n + 1) * HID, :], preferred_element_type=F32)
        total = part if total is None else total + part
    out_ref[...] = total.astype(BF16)


def down_of(me, pieces, w):
    return pl.pallas_call(
        down_kernel,
        out_shape=jax.ShapeDtypeStruct((SLOTS, WIDTH), BF16),
        in_specs=[SCALAR] + [full()] * 4 + [HERE],
        out_specs=whole((SLOTS, WIDTH)),
        scratch_shapes=[pltpu.VMEM((ALL_HID, WIDTH), BF16), pltpu.SemaphoreType.DMA((4,))],
        name="down",
        compiler_params=limit(58),
    )(me, *pieces, w)


def combine_kernel(sel_ref, weight_ref, x_ref, out_ref):
    x = x_ref[...]
    first = jnp.dot(sel_ref[0], x, preferred_element_type=F32)
    second = jnp.dot(sel_ref[1], x, preferred_element_type=F32)
    for c in range(WIDTH // BLOCK):
        cols = slice(c * BLOCK, (c + 1) * BLOCK)
        out_ref[:, cols] = (
            weight_ref[0] * first[:, cols] + weight_ref[1] * second[:, cols]
        ).astype(BF16)


def combine(sel, weight, x):
    return pl.pallas_call(
        combine_kernel,
        out_shape=jax.ShapeDtypeStruct((TOK, WIDTH), BF16),
        in_specs=[whole((2, TOK, SLOTS)), whole((2, TOK, TOK)), full()],
        out_specs=full(),
        name="combine",
        compiler_params=limit(58),
    )(sel, weight, x)


def shift(x, step):
    return lax.ppermute(x, "tensor", [(i, (i + step) % 4) for i in range(4)])


def exchange(x):
    sized = x.reshape(N_EXP, CAP, x.shape[1])
    got = lax.all_to_all(sized, "seq", split_axis=0, concat_axis=0, tiled=True)
    return got.reshape(x.shape)


def local(
    hidden_in,
    norm_gain,
    expert_ids,
    gate_weights,
    w_gate,
    w_up,
    w_down,
    scale_gate,
    scale_up,
    scale_down,
):
    me = lax.axis_index("tensor").astype(jnp.int32).reshape(1)
    ids = expert_ids.T
    send, q, picker = source(ids, hidden_in, norm_gain)
    q_pieces = (q, near(shift(q, 1)), near(shift(q, 3)), near(shift(q, 2)))
    mine = exchange(send)
    routed = route(picker, q_pieces)
    got_q = near(exchange(routed))
    low = near(shift(mine, 1))
    high = near(shift(mine, 3))
    far_low = near(shift(rows_of(low, 0), 1))
    far_high = near(shift(rows_of(high, HALF), 3))
    w_both = dequant_up(scale_gate[0].T, scale_up[0].T, w_gate[0], w_up[0])
    w_out = dequant_down(scale_down[0], w_down[0])
    sel, weight = combine_prep(ids, gate_weights.T, picker)
    acc = first_part(me, near(mine), low, high, w_both)
    hidden = hidden_of(me, got_q, far_low, far_high, acc, w_both)
    others = tuple(near(shift(hidden, step)) for step in (1, 3, 2))
    outputs = down_of(me, (hidden,) + others, w_out)
    returned = exchange(outputs)
    return combine(sel, weight, near(returned))


def solution(mesh):
    in_specs = (
        P(("dp", "seq"), "tensor"),
        P("tensor"),
        P(("dp", "seq"), None),
        P(("dp", "seq"), None),
        P("seq", None, "tensor"),
        P("seq", None, "tensor"),
        P("seq", None, "tensor"),
        P("seq", None, "tensor"),
        P("seq", None, "tensor"),
        P("seq", None, "tensor"),
    )
    out_specs = P(("dp", "seq"), "tensor")
    return jax.shard_map(local, mesh=mesh, in_specs=in_specs, out_specs=out_specs, check_vma=False)
```
